32 devices in a mesh: ctx: 8 (over z, core), wt: 4 (over y, x).
Axes of the slice: x: 2, y: 2, z: 4, core: 2. Of those that a mesh axis runs over, the one named last changes fastest.
Arguments:
- tokens: bfloat16 [4, 2048, 1024], P('wt', 'ctx'), may hold values from -6 to 6
- cotangent: bfloat16 [4, 2048, 1024], P('wt', 'ctx'), may hold values from -6 to 6
- ln1_gain: bfloat16 [1024], P('wt'), may hold values from 0.25 to 1.75
- ln1_bias: bfloat16 [1024], P('wt'), may hold values from -3 to 3
- w_qkv: bfloat16 [1024, 3072], P('wt'), may hold values from -0.1875 to 0.1875
- bias_q: bfloat16 [1024], P('wt'), may hold values from -3 to 3
- bias_v: bfloat16 [1024], P('wt'), may hold values from -1.25 to 1.25
- w_out: bfloat16 [1024, 1024], P('wt'), may hold values from -0.75 to 0.75
- bias_out: bfloat16 [1024], P('wt'), may hold values from -3 to 3
- ln2_gain: bfloat16 [1024], P('wt'), may hold values from 0.25 to 1.75
- ln2_bias: bfloat16 [1024], P('wt'), may hold values from -3 to 3
- w_up: bfloat16 [1024, 4096], P('wt'), may hold values from -0.1875 to 0.1875
- bias_up: bfloat16 [4096], P('wt'), may hold values from -3 to 3
- w_down: bfloat16 [4096, 1024], P('wt'), may hold values from -0.09375 to 0.09375
- bias_down: bfloat16 [1024], P('wt'), may hold values from -3 to 3
Outputs:
- out: bfloat16 [4, 2048, 1024], P('wt', 'ctx')
- grad_tokens: float32 [4, 2048, 1024], P('wt', 'ctx')
- grad_ln1_gain: float32 [1024], P('wt')
- grad_ln1_bias: float32 [1024], P('wt')
- grad_w_qkv: float32 [1024, 3072], P('wt')
- grad_bias_q: float32 [1024], P('wt')
- grad_bias_v: float32 [1024], P('wt')
- grad_w_out: float32 [1024, 1024], P('wt')
- grad_bias_out: float32 [1024], P('wt')
- grad_ln2_gain: float32 [1024], P('wt')
- grad_ln2_bias: float32 [1024], P('wt')
- grad_w_up: float32 [1024, 4096], P('wt')
- grad_bias_up: float32 [4096], P('wt')
- grad_w_down: float32 [4096, 1024], P('wt')
- grad_bias_down: float32 [1024], P('wt')
The draws below stay inside these ranges and needn't reach their ends.
All inputs are finite; a program needn't handle non-finite values.
Results may differ from the reference program's by a relative error of at most 0.02.
Values may be sent and summed in bfloat16 or wider, within the bound.
A program may use at most 192 MiB of HBM per device.

```python
from functools import partial
import jax
import jax.numpy as jnp
from jax import lax

D = 1024
HEADS = 16
HEAD_DIM = 64
FF = 4096
TOK_DEV = 256
BLK = 128
LEN = 2048
SEQS = 4
N_CTX = 8


def block_levels(key, dims, split, low, top_value):
    factor_of = 1.0
    for position, blocks in split:
        draws = jax.random.uniform(jax.random.fold_in(jax.random.fold_in(key, 6), position), (blocks,), jnp.float32, low / len(split), top_value / len(split))
        factor_of = factor_of * jnp.repeat(jnp.exp(draws), dims[position] // blocks).reshape((-1,) + (1,) * (len(dims) - 1 - position))
    return factor_of


def noise(key, shape, scale, most, cuts=(), kind=jnp.bfloat16):
    factor_of = block_levels(key, shape, cuts, -0.22, 0.18) if cuts else 1.0
    entries = jax.random.normal(key, shape, jnp.float32) * scale * factor_of
    return jnp.minimum(jnp.maximum(entries, -most), most).astype(kind)


def setup_inputs(seed: int = 0) -> dict:
    key_of = jax.random.split(jax.random.key(seed), 16)
    return {
        "tokens": noise(key_of[0], (SEQS, LEN, D), 1.0, 6.0, ((0, 4), (1, 8))),
        "cotangent": noise(key_of[1], (SEQS, LEN, D), 1.0, 6.0, ((0, 4), (1, 8))),
        "ln1_gain": jnp.clip(1.0 + 0.15 * jax.random.normal(key_of[2], (D,), jnp.float32), 0.25, 1.75).astype(jnp.bfloat16),
        "ln1_bias": noise(key_of[3], (D,), 0.5, 3.0, ((0, 4),)),
        "w_qkv": noise(key_of[4], (D, 3 * D), D ** -0.5, 0.1875, ((0, 4),)),
        "bias_q": noise(key_of[5], (D,), 0.5, 3.0, ((0, 4),)),
        "bias_v": noise(key_of[6], (D,), 0.2, 1.25, ((0, 4),)),
        "w_out": noise(key_of[7], (D, D), (D // 16) ** -0.5, 0.75, ((0, 4),)),
        "bias_out": noise(key_of[8], (D,), 0.5, 3.0, ((0, 4),)),
        "ln2_gain": jnp.clip(1.0 + 0.15 * jax.random.normal(key_of[9], (D,), jnp.float32), 0.25, 1.75).astype(jnp.bfloat16),
        "ln2_bias": noise(key_of[10], (D,), 0.5, 3.0, ((0, 4),)),
        "w_up": noise(key_of[11], (D, FF), D ** -0.5, 0.1875, ((0, 4),)),
        "bias_up": noise(key_of[12], (FF,), 0.5, 3.0, ((0, 4),)),
        "w_down": noise(key_of[13], (FF, D), FF ** -0.5, 0.09375, ((0, 4),)),
        "bias_down": noise(key_of[14], (D,), 0.5, 3.0, ((0, 4),)),
    }


EPSILON = 1e-05
MASKED_SCORE = -1e+30

@jax.custom_vjp
def low(v):
    return lax.optimization_barrier(v.astype(jnp.bfloat16)).astype(jnp.float32)

@jax.custom_vjp
def low_back(v):
    return v

def low_keep(v):
    return (low(v), None)

def low_pass(kept, grad):
    return (grad,)

def back_keep(v):
    return (v, None)

def back_low(kept, grad):
    return (low(grad),)
low.defvjp(low_keep, low_pass)
low_back.defvjp(back_keep, back_low)

def norm_rows(values_in, gain, shift):
    mean_val = lax.optimization_barrier(jnp.mean(values_in, axis=-1, keepdims=True))
    centred = values_in - mean_val
    spread = lax.optimization_barrier(jnp.mean(centred * centred, axis=-1, keepdims=True))
    return centred * lax.rsqrt(spread + EPSILON) * gain + shift

def gelu_tanh(values_in):
    return jax.nn.gelu(values_in, approximate=True)

def product_high(left, right):
    return jnp.dot(left, right, precision=lax.Precision.HIGHEST)

def attention(query_rows, key_rows, value_rows, positions):
    length = query_rows.shape[0]
    block_rows = min(512, length)
    query_blocks = query_rows.reshape(length // block_rows, block_rows, HEADS, HEAD_DIM)
    pos_blocks = positions.reshape(length // block_rows, block_rows)

    def one_block(pair_in):
        query_block, query_pos = pair_in
        scores = jnp.einsum('qhd,khd->hqk', query_block, key_rows, precision=lax.Precision.HIGHEST) * HEAD_DIM ** (-0.5)
        scores = low_back(scores)
        scores = jnp.where(positions[None, None, :] <= query_pos[None, :, None], scores, MASKED_SCORE)
        log_norm = jax.scipy.special.logsumexp(scores, axis=-1, keepdims=True)
        prob_low = low(jnp.exp(scores - log_norm))
        return jnp.einsum('hqk,khd->qhd', prob_low, value_rows, precision=lax.Precision.HIGHEST)
    attended = lax.map(jax.checkpoint(one_block), (query_blocks, pos_blocks))
    return attended.reshape(length, HEADS * HEAD_DIM)

def layer(params, inputs, positions):
    gain_one, shift_one, whole_qkv, query_bias, value_bias, whole_out, out_bias, gain_two, shift_two, whole_up, up_bias, whole_down, down_bias = params
    width = inputs.shape[1]
    normed_one = low(norm_rows(inputs, gain_one, shift_one))
    qkv_bias = jnp.concatenate([query_bias, jnp.zeros_like(query_bias), value_bias])
    qkv_rows = low_back(low(product_high(normed_one, whole_qkv) + qkv_bias))
    query_rows = qkv_rows[:, :width].reshape(-1, HEADS, HEAD_DIM)
    key_rows = qkv_rows[:, width:2 * width].reshape(-1, HEADS, HEAD_DIM)
    value_rows = qkv_rows[:, 2 * width:].reshape(-1, HEADS, HEAD_DIM)
    attended = low_back(low(attention(query_rows, key_rows, value_rows, positions)))
    mixed_attn = low_back(product_high(attended, whole_out) + out_bias)
    resid_mid = inputs + mixed_attn
    normed_two = low(norm_rows(resid_mid, gain_two, shift_two))
    hidden_pre = low_back(product_high(normed_two, whole_up) + up_bias)
    hidden_low = low(gelu_tanh(hidden_pre))
    return resid_mid + product_high(hidden_low, whole_down) + down_bias

def reference(tokens, cotangent, ln1_gain, ln1_bias, w_qkv, bias_q, bias_v, w_out, bias_out, ln2_gain, ln2_bias, w_up, bias_up, w_down, bias_down):
    rows_all = jnp.arange(LEN, dtype=jnp.int32)
    device_of = rows_all // TOK_DEV
    half_of = rows_all // BLK % 2
    block_of = jnp.where(half_of == 0, device_of, 2 * N_CTX - 1 - device_of)
    positions = (block_of * BLK + rows_all % BLK).astype(jnp.int32)
    params = tuple((weight.astype(jnp.float32) for weight in (ln1_gain, ln1_bias, w_qkv, bias_q, bias_v, w_out, bias_out, ln2_gain, ln2_bias, w_up, bias_up, w_down, bias_down)))
    forward = partial(layer, positions=positions)

    def one_sequence(totals, pair_in):
        seq_tokens, seq_grad = pair_in
        result, pullback = jax.vjp(forward, params, seq_tokens.astype(jnp.float32))
        grad_params, grad_inputs = pullback(seq_grad.astype(jnp.float32))
        totals = jax.tree.map(jnp.add, totals, grad_params)
        return (totals, (result.astype(jnp.bfloat16), grad_inputs))
    initial = tuple((jnp.zeros_like(weight) for weight in params))
    totals, (out, grad_tokens) = lax.scan(one_sequence, initial, (tokens, cotangent))
    return (out, grad_tokens, totals[0], totals[1], totals[2], totals[3], totals[4], totals[5], totals[6], totals[7], totals[8], totals[9], totals[10], totals[11], totals[12])
```

```python
import functools

import jax
import jax.numpy as jnp
import numpy as np
from jax import lax
from jax.experimental import pallas as pl
from jax.experimental.pallas import tpu as pltpu
from jax.sharding import Mesh
from jax.sharding import PartitionSpec as P

HEADS = 16
HEAD_DIM = 64


EPSILON = 1e-05
MASKED_SCORE = -1e30
Q_TILE = 256
K_TILE = 512


def norm_rows(values_in, gain, shift):
    mean_val = jnp.mean(values_in, axis=-1, keepdims=True)
    centred = values_in - mean_val
    spread = jnp.mean(centred * centred, axis=-1, keepdims=True)
    return centred * lax.rsqrt(spread + EPSILON) * gain + shift


def gelu_tanh(values_in):
    return jax.nn.gelu(values_in, approximate=True)


def product(left, right):
    return jnp.dot(left, right, preferred_element_type=jnp.float32)


def product_left(left, right):
    return lax.dot_general(
        left, right, (((0,), (0,)), ((), ())), preferred_element_type=jnp.float32
    )


def product_right(left, right):
    return lax.dot_general(
        left, right, (((1,), (1,)), ((), ())), preferred_element_type=jnp.float32
    )


def tile_allowed(q_start, k_start):
    q_pos = q_start + lax.broadcasted_iota(jnp.int32, (Q_TILE, K_TILE), 0)
    k_pos = k_start + lax.broadcasted_iota(jnp.int32, (Q_TILE, K_TILE), 1)
    return k_pos <= q_pos


def attend_kernel(heads, qkv_ref, att_ref, lse_ref):
    width = heads * HEAD_DIM
    q_start = pl.multiple_of(pl.program_id(0) * Q_TILE, Q_TILE)
    q_rows = pl.ds(q_start, Q_TILE)
    scale = HEAD_DIM ** (-0.5)
    queries = [
        qkv_ref[q_rows, h * HEAD_DIM : (h + 1) * HEAD_DIM] * jnp.bfloat16(scale)
        for h in range(heads)
    ]

    def step(j, carried):
        k_start = pl.multiple_of(j * K_TILE, K_TILE)
        k_rows = pl.ds(k_start, K_TILE)
        allowed = tile_allowed(q_start, k_start)
        new = []
        for h in range(heads):
            peak, total, acc = carried[h]
            at = width + h * HEAD_DIM
            keys = qkv_ref[k_rows, at : at + HEAD_DIM]
            values = qkv_ref[k_rows, at + width : at + width + HEAD_DIM]
            scores = jnp.where(allowed, product_right(queries[h], keys), MASKED_SCORE)
            peak_new = jnp.maximum(peak, jnp.max(scores, axis=-1, keepdims=True))
            fade = jnp.exp(peak - peak_new)
            prob = jnp.exp(scores - peak_new)
            total = total * fade + jnp.sum(prob, axis=-1, keepdims=True)
            acc = acc * fade + product(prob.astype(jnp.bfloat16), values)
            new.append((peak_new, total, acc))
        return tuple(new)

    empty = (
        jnp.full((Q_TILE, 1), MASKED_SCORE, jnp.float32),
        jnp.zeros((Q_TILE, 1), jnp.float32),
        jnp.zeros((Q_TILE, HEAD_DIM), jnp.float32),
    )
    steps = (q_start + Q_TILE + K_TILE - 1) // K_TILE
    done = lax.fori_loop(0, steps, step, (empty,) * heads)
    for h in range(heads):
        peak, total, acc = done[h]
        att_ref[:, h * HEAD_DIM : (h + 1) * HEAD_DIM] = acc / total
        lse_ref[:, h : h + 1] = peak + jnp.log(total)


def attend_back_kernel(heads, qkv_ref, grad_ref, att_ref, lse_ref, out_ref, keys_acc, values_acc):
    width = heads * HEAD_DIM
    index = pl.program_id(0)
    q_start = pl.multiple_of(index * Q_TILE, Q_TILE)
    q_rows = pl.ds(q_start, Q_TILE)
    scale = HEAD_DIM ** (-0.5)

    @pl.when(index == 0)
    def _():
        keys_acc[...] = jnp.zeros_like(keys_acc)
        values_acc[...] = jnp.zeros_like(values_acc)

    queries, grads, norms, deltas = [], [], [], []
    for h in range(heads):
        cols = slice(h * HEAD_DIM, (h + 1) * HEAD_DIM)
        queries.append(qkv_ref[q_rows, cols] * jnp.bfloat16(scale))
        grad = grad_ref[:, cols]
        grads.append(grad)
        norms.append(lse_ref[:, h : h + 1])
        deltas.append(
            jnp.sum(grad.astype(jnp.float32) * att_ref[:, cols], axis=-1, keepdims=True)
        )

    def step(j, carried):
        k_start = pl.multiple_of(j * K_TILE, K_TILE)
        k_rows = pl.ds(k_start, K_TILE)
        allowed = tile_allowed(q_start, k_start)
        new = []
        for h in range(heads):
            cols = slice(h * HEAD_DIM, (h + 1) * HEAD_DIM)
            at = width + h * HEAD_DIM
            keys = qkv_ref[k_rows, at : at + HEAD_DIM]
            values = qkv_ref[k_rows, at + width : at + width + HEAD_DIM]
            scores = jnp.where(allowed, product_right(queries[h], keys), MASKED_SCORE)
            prob = jnp.exp(scores - norms[h])
            grad_prob = product_right(grads[h], values)
            grad_score = (prob * (grad_prob - deltas[h])).astype(jnp.bfloat16)
            values_acc[k_rows, cols] += product_left(prob.astype(jnp.bfloat16), grads[h])
            keys_acc[k_rows, cols] += product_left(grad_score, queries[h])
            new.append(carried[h] + product(grad_score, keys))
        return tuple(new)

    steps = (q_start + Q_TILE + K_TILE - 1) // K_TILE
    zero = jnp.zeros((Q_TILE, HEAD_DIM), jnp.float32)
    done = lax.fori_loop(0, steps, step, (zero,) * heads)
    for h in range(heads):
        out_ref[q_rows, h * HEAD_DIM : (h + 1) * HEAD_DIM] = (done[h] * scale).astype(
            jnp.bfloat16
        )

    @pl.when(index == pl.num_programs(0) - 1)
    def _():
        out_ref[:, width : 2 * width] = keys_acc[...].astype(jnp.bfloat16)
        out_ref[:, 2 * width :] = values_acc[...].astype(jnp.bfloat16)


def attend(qkv, heads):
    rows, width = qkv.shape[0], heads * HEAD_DIM
    work = rows * rows // 2 * heads
    return pl.pallas_call(
        functools.partial(attend_kernel, heads),
        grid=(rows // Q_TILE,),
        in_specs=[pl.BlockSpec((rows, 3 * width), lambda i: (0, 0))],
        out_specs=[
            pl.BlockSpec((Q_TILE, width), lambda i: (i, 0)),
            pl.BlockSpec((Q_TILE, heads), lambda i: (i, 0)),
        ],
        out_shape=[
            jax.ShapeDtypeStruct((rows, width), jnp.float32),
            jax.ShapeDtypeStruct((rows, heads), jnp.float32),
        ],
        compiler_params=pltpu.CompilerParams(vmem_limit_bytes=40 << 20),
        cost_estimate=pl.CostEstimate(
            flops=work * 1024, bytes_accessed=rows * width * 10, transcendentals=work
        ),
    )(qkv)


def attend_back(qkv, grad, att, lse, heads):
    rows, width = qkv.shape[0], heads * HEAD_DIM
    work = rows * rows // 2 * heads
    return pl.pallas_call(
        functools.partial(attend_back_kernel, heads),
        grid=(rows // Q_TILE,),
        in_specs=[
            pl.BlockSpec((rows, 3 * width), lambda i: (0, 0)),
            pl.BlockSpec((Q_TILE, width), lambda i: (i, 0)),
            pl.BlockSpec((Q_TILE, width), lambda i: (i, 0)),
            pl.BlockSpec((Q_TILE, heads), lambda i: (i, 0)),
        ],
        out_specs=pl.BlockSpec((rows, 3 * width), lambda i: (0, 0)),
        out_shape=jax.ShapeDtypeStruct((rows, 3 * width), jnp.bfloat16),
        scratch_shapes=[
            pltpu.VMEM((rows, width), jnp.float32),
            pltpu.VMEM((rows, width), jnp.float32),
        ],
        compiler_params=pltpu.CompilerParams(vmem_limit_bytes=40 << 20),
        cost_estimate=pl.CostEstimate(
            flops=work * 2560, bytes_accessed=rows * width * 20, transcendentals=work
        ),
    )(qkv, grad, att, lse)


def swap(value):
    return lax.ppermute(value, "core", [(0, 1), (1, 0)])


def pair_stack(own, core):
    other = swap(own)
    first = core == 0
    return jnp.stack([jnp.where(first, own, other), jnp.where(first, other, own)])


def pair_sum(partial, core):
    own = lax.dynamic_index_in_dim(partial, core, 0, keepdims=False)
    other = lax.dynamic_index_in_dim(partial, 1 - core, 0, keepdims=False)
    return own + swap(other.astype(jnp.bfloat16)).astype(jnp.float32)


def to_positions(stored, devices, block):
    parts = stored.reshape(devices, 2, block, -1)
    return jnp.concatenate([parts[:, 0], parts[::-1, 1]]).reshape(stored.shape)


def to_stored(ordered, devices, block):
    parts = ordered.reshape(2, devices, block, -1)
    return jnp.stack([parts[0], parts[1, ::-1]], axis=1).reshape(ordered.shape)


def exchange(value):
    return lax.all_to_all(value, "z", split_axis=0, concat_axis=0, tiled=False)


def per_device(
    tokens,
    cotangent,
    ln1_gain,
    ln1_bias,
    w_qkv,
    bias_q,
    bias_v,
    w_out,
    bias_out,
    ln2_gain,
    ln2_bias,
    w_up,
    bias_up,
    w_down,
    bias_down,
):
    core = lax.axis_index("core")
    shards = lax.axis_size("wt")
    chips = lax.axis_size("z")
    devices = 2 * chips
    inputs = tokens[0].astype(jnp.float32)
    tok_count, width = inputs.shape
    block = tok_count // 2
    half = width // 2
    shard = width // shards
    hidden = w_up.shape[1] // 2
    heads = HEADS // devices
    cols = heads * HEAD_DIM

    def half_of(value, axis):
        return lax.dynamic_index_in_dim(value, core, axis, keepdims=False)

    def gather(value):
        return lax.all_gather(value, "wt", axis=0, tiled=True)

    vectors = [ln1_gain, ln1_bias, bias_q, bias_v, bias_out, ln2_gain, ln2_bias, bias_down, bias_up]
    sizes = [v.shape[0] for v in vectors]
    cuts = [sum(sizes[:i]) for i in range(len(sizes) + 1)]
    packed = lax.all_gather(jnp.concatenate(vectors), "wt", axis=0)
    whole = [
        packed[:, a:b].reshape(-1).astype(jnp.float32) for a, b in zip(cuts[:-1], cuts[1:])
    ]
    gain_one, shift_one, query_bias, value_bias, out_bias = whole[:5]
    gain_two, shift_two, down_bias, up_bias = whole[5:]
    query_bias = half_of(query_bias.reshape(shards, 2, -1), 1).reshape(-1)
    value_bias = half_of(value_bias.reshape(shards, 2, -1), 1).reshape(-1)
    up_bias = half_of(up_bias.reshape(shards, 2, -1), 1).reshape(-1)

    half_qkv = gather(half_of(w_qkv.reshape(shard, 3, shards, 2, shard // 2), 3).reshape(shard, -1))
    half_out = gather(half_of(w_out.reshape(2, shard // 2, width), 0))
    half_up = gather(half_of(w_up.reshape(shard, shards, 2, -1), 2).reshape(shard, -1))
    half_down = gather(half_of(w_down.reshape(2, -1, width), 0))

    normed_low = norm_rows(inputs, gain_one, shift_one).astype(jnp.bfloat16)
    normed_pair = pair_stack(normed_low, core).reshape(2 * tok_count, width)
    grad_rows = cotangent[0]
    grad_float = grad_rows.astype(jnp.float32)
    grad_pair = jnp.concatenate([grad_rows, swap(grad_rows)])
    qkv_bias = jnp.concatenate([query_bias, jnp.zeros_like(query_bias), value_bias])
    qkv_rows = (product(normed_pair, half_qkv) + qkv_bias).astype(jnp.bfloat16)
    qkv_sent = jnp.transpose(
        qkv_rows.reshape(2 * tok_count, 3, chips, cols), (2, 0, 1, 3)
    ).reshape(chips, 2 * tok_count, 3 * cols)
    qkv = to_positions(exchange(qkv_sent).reshape(-1, 3 * cols), devices, block)
    attended, log_norm = attend(qkv, heads)
    att_sent = to_stored(attended.astype(jnp.bfloat16), devices, block)
    att_back = exchange(att_sent.reshape(chips, 2 * tok_count, cols))
    att_low = jnp.transpose(att_back, (1, 0, 2)).reshape(2 * tok_count, half)
    mixed = product(att_low, half_out).reshape(2, tok_count, width)
    resid_mid = inputs + pair_sum(mixed, core) + out_bias
    normed_two_low = norm_rows(resid_mid, gain_two, shift_two).astype(jnp.bfloat16)
    two_pair = jnp.concatenate([normed_two_low, swap(normed_two_low)])
    hidden_pre = product(two_pair, half_up) + up_bias
    hidden_act, gelu_back = jax.vjp(gelu_tanh, hidden_pre)
    hidden_low = hidden_act.astype(jnp.bfloat16)
    grad_down = product_left(hidden_low, grad_pair).astype(jnp.bfloat16)
    grad_down = lax.psum_scatter(grad_down, "wt", scatter_dimension=0, tiled=True)
    grad_pre = gelu_back(product_right(grad_pair, half_down))[0].astype(jnp.bfloat16)
    grad_up = product_left(two_pair, grad_pre).astype(jnp.bfloat16)
    grad_up = lax.psum_scatter(grad_up, "wt", scatter_dimension=0, tiled=True)
    grad_up_bias = jnp.sum(grad_pre.astype(jnp.float32), axis=0)
    down_part = product(hidden_low, half_down)
    result_rows = (
        resid_mid
        + down_part[:tok_count]
        + swap(down_part[tok_count:].astype(jnp.bfloat16)).astype(jnp.float32)
        + down_bias
    )
    out = result_rows.astype(jnp.bfloat16)[None]
    back_part = product_right(grad_pre, half_up)
    grad_normed_two = back_part[:tok_count] + swap(
        back_part[tok_count:].astype(jnp.bfloat16)
    ).astype(jnp.float32)
    norm_two_out, norm_two_back = jax.vjp(norm_rows, resid_mid, gain_two, shift_two)
    grad_mid_norm, grad_gain_two, grad_shift_two = norm_two_back(grad_normed_two)
    grad_mid = grad_float + grad_mid_norm
    grad_mix_low = grad_mid.astype(jnp.bfloat16)
    mix_pair = pair_stack(grad_mix_low, core).reshape(2 * tok_count, width)
    grad_att_low = product_right(mix_pair, half_out).astype(jnp.bfloat16)
    grad_out = product_left(att_low, mix_pair).astype(jnp.bfloat16)
    grad_out = lax.psum_scatter(grad_out, "wt", scatter_dimension=0, tiled=True)
    grad_att_sent = jnp.transpose(grad_att_low.reshape(2 * tok_count, chips, cols), (1, 0, 2))
    grad_att = to_positions(exchange(grad_att_sent).reshape(-1, cols), devices, block)
    grad_heads = attend_back(qkv, grad_att, attended, log_norm, heads)
    grad_sent = to_stored(grad_heads, devices, block)
    grad_back = exchange(grad_sent.reshape(chips, 2 * tok_count, 3 * cols))
    grad_qkv = jnp.transpose(
        grad_back.reshape(chips, 2 * tok_count, 3, cols), (1, 2, 0, 3)
    ).reshape(2 * tok_count, 3 * half)
    grad_normed_one = pair_sum(
        product_right(grad_qkv, half_qkv).reshape(2, tok_count, width), core
    )
    norm_one_out, norm_one_back = jax.vjp(norm_rows, inputs, gain_one, shift_one)
    grad_in_norm, grad_gain_one, grad_shift_one = norm_one_back(grad_normed_one)
    grad_inputs = (grad_mid + grad_in_norm)[None]
    grad_qkv_weight = product_left(normed_pair, grad_qkv).astype(jnp.bfloat16)
    qkv_sums = jnp.sum(grad_qkv.astype(jnp.float32), axis=0)

    def half_in(value):
        value = value.reshape(shards, 1, -1)
        mask = jnp.arange(2).reshape(1, 2, 1) == core
        return jnp.where(mask, value, 0.0)

    vector_grads = [
        grad_gain_one,
        grad_shift_one,
        half_in(qkv_sums[:half]),
        half_in(qkv_sums[2 * half :]),
        jnp.sum(grad_mix_low.astype(jnp.float32), axis=0),
        grad_gain_two,
        grad_shift_two,
        jnp.sum(grad_float, axis=0),
        half_in(grad_up_bias),
    ]
    vector_rows = jnp.concatenate([v.reshape(shards, -1) for v in vector_grads], axis=1)
    pad_rows = 16 * (-(-cuts[-1] // (16 * 3 * half)))
    vector_rows = jnp.pad(vector_rows, ((0, 0), (0, pad_rows * 3 * half - cuts[-1])))
    last = jnp.concatenate(
        [
            grad_qkv_weight.reshape(shards, shard, 3 * half),
            vector_rows.reshape(shards, pad_rows, 3 * half).astype(jnp.bfloat16),
        ],
        axis=1,
    ).reshape(-1, 3 * half)
    last = lax.psum_scatter(last, "wt", scatter_dimension=0, tiled=True)
    grad_down, grad_up, grad_out, last = lax.psum((grad_down, grad_up, grad_out, last), "z")
    own_vector = last[shard:]
    vector = (own_vector.astype(jnp.float32) + swap(own_vector).astype(jnp.float32)).reshape(-1)
    vector_out = [vector[a:b] for a, b in zip(cuts[:-1], cuts[1:])]

    def both(value):
        return pair_stack(value, core).astype(jnp.float32)

    down_out = both(grad_down).reshape(-1, width)
    out_out = both(grad_out).reshape(-1, width)
    up_out = jnp.moveaxis(both(grad_up).reshape(2, shard, shards, -1), 0, 2).reshape(shard, -1)
    qkv_out = jnp.moveaxis(
        both(last[:shard]).reshape(2, shard, 3, shards, shard // 2), 0, 3
    ).reshape(shard, -1)
    return (
        out,
        grad_inputs,
        vector_out[0],
        vector_out[1],
        qkv_out,
        vector_out[2],
        vector_out[3],
        out_out,
        vector_out[4],
        vector_out[5],
        vector_out[6],
        up_out,
        vector_out[8],
        down_out,
        vector_out[7],
    )


def solution(mesh):
    count = mesh.shape["ctx"]
    split = Mesh(
        np.asarray(mesh.devices).reshape(count // 2, 2, mesh.shape["wt"]), ("z", "core", "wt")
    )
    return jax.shard_map(
        per_device,
        mesh=split,
        in_specs=(
            P("wt", ("z", "core"), None),
            P("wt", ("z", "core"), None),
            P("wt"),
            P("wt"),
            P("wt", None),
            P("wt"),
            P("wt"),
            P("wt", None),
            P("wt"),
            P("wt"),
            P("wt"),
            P("wt", None),
            P("wt"),
            P("wt", None),
            P("wt"),
        ),
        out_specs=(
            P("wt", ("z", "core"), None),
            P("wt", ("z", "core"), None),
            P("wt"),
            P("wt"),
            P("wt", None),
            P("wt"),
            P("wt"),
            P("wt", None),
            P("wt"),
            P("wt"),
            P("wt"),
            P("wt", None),
            P("wt"),
            P("wt", None),
            P("wt"),
        ),
        check_vma=False,
    )
```
